256 devices in a mesh: section: 32 (over x, z), dp: 8 (over y, core).
Axes of the slice: x: 4, y: 4, z: 8, core: 2. Of those that a mesh axis runs over, the one named last changes fastest.
Arguments:
- inputs: bfloat16 [8, 256, 512], P(None, 'dp'), may hold values from -6 to 6
- targets: bfloat16 [8, 256, 512], P(None, 'dp'), may hold values from -6 to 6
- w_in: bfloat16 [32, 512, 4096], P('section'), may hold values from -0.25 to 0.25
- w_out: bfloat16 [32, 4096, 512], P('section'), may hold values from -0.0234375 to 0.0234375
Outputs:
- grad_w_in: float32 [32, 512, 4096], P('section', None, 'dp')
- grad_w_out: float32 [32, 4096, 512], P('section', 'dp')
The draws below stay inside these ranges and needn't reach their ends.
All inputs are finite; a program needn't handle non-finite values.
Results may differ from the reference program's by a relative error of at most 0.019.
Values may be sent and summed in bfloat16 or wider, within the bound.
No kernel may reach another device: no remote copies, remote signals or barrier semaphores. Data moves between devices by JAX's collectives and lax.ppermute only.
A program may use at most 64 MiB of HBM per device.

```python
import math
import jax
import jax.numpy as jnp
from jax import lax

D = 512
FF = 4096
MICRO = 8
SECTIONS = 32
BROWS = 256


def spiked(values, own_key, source, target, shards_of, factor):
    owner, partner = [(jnp.arange(values.shape[dim]) // (values.shape[dim] // shards_of)).reshape([-1 if axis == dim else 1 for axis in range(values.ndim)]) for dim in (source, target)]
    chosen = jax.random.permutation(own_key, shards_of)[partner]
    strong = (owner == chosen) | (owner == (partner + shards_of // 2) % shards_of)
    return jnp.where(strong, factor * values, values)


def block_scale(rng, dims, shards, least, high):
    def one(dim, parts):
        draws = jax.random.uniform(jax.random.fold_in(jax.random.fold_in(rng, 6), dim), (parts,), jnp.float32, least / len(shards), high / len(shards))
        return jnp.repeat(jnp.exp(draws), dims[dim] // parts).reshape((-1,) + (1,) * (len(dims) - dim - 1))

    gain = one(*shards[0])
    for cut in shards[1:]:
        gain = gain * one(*cut)
    return gain


def normal_values(stream_key, extent, deviation, bound, pieces=(), kind=jnp.bfloat16):
    drawn = jax.random.normal(stream_key, extent, jnp.float32) * deviation
    if len(pieces) > 0:
        drawn = block_scale(stream_key, extent, pieces, -0.22, 0.18) * drawn
    return jnp.clip(drawn, min=-bound, max=bound).astype(kind)


def noise_with(rng, extent, width, bound, shards, heavy, dtype=jnp.bfloat16):
    drawn = width * jax.random.normal(rng, extent, jnp.float32)
    if shards:
        drawn = drawn * block_scale(rng, extent, shards, -0.22, 0.18)
    return jnp.clip(spiked(drawn, jax.random.fold_in(rng, 3), *heavy), -bound, bound).astype(dtype)


def setup_inputs(seed: int = 0) -> dict:
    key_of = jax.random.split(jax.random.key(seed), 5)
    inputs = noise_with(key_of[0], (MICRO, BROWS, D), 1.0, 6.0, ((1, 8),), (1, 2, 8, 2.0))
    targets = normal_values(key_of[1], (MICRO, BROWS, D), 1.0, 6.0, ((1, 8),))
    w_in = normal_values(key_of[2], (SECTIONS, D, FF), D ** -0.5, 0.25, ((0, 32),))
    w_out = normal_values(key_of[3], (SECTIONS, FF, D), (16 * FF) ** -0.5, 0.0234375, ((0, 32),))
    return {"inputs": inputs, "targets": targets, "w_in": w_in, "w_out": w_out}


def cell_forward(act_in, weight_in, weight_out):
    pre_act = jnp.dot(act_in, weight_in, preferred_element_type=jnp.float32)
    hidden = (pre_act * jax.nn.sigmoid(pre_act)).astype(jnp.bfloat16)
    act_out = (act_in.astype(jnp.float32) + jnp.dot(hidden, weight_out, preferred_element_type=jnp.float32)).astype(jnp.bfloat16)
    return (hidden, act_out)

def cell_backward(act_in, hidden, grad_y, weight_in, weight_out):
    pre_act = jnp.dot(act_in, weight_in, preferred_element_type=jnp.float32)
    sigma = jax.nn.sigmoid(pre_act)
    slope = sigma + pre_act * sigma * (1.0 - sigma)
    hidden_f = hidden.astype(jnp.float32)
    grad_f = grad_y.astype(jnp.float32)
    grad_out = jnp.einsum('rf,rd->fd', hidden_f, grad_f)
    through = jnp.einsum('rd,fd->rf', grad_f, weight_out.astype(jnp.float32))
    grad_pre = (through * slope).astype(jnp.bfloat16)
    grad_in = jnp.einsum('rd,rf->df', act_in.astype(jnp.float32), grad_pre.astype(jnp.float32))
    grad_x = (grad_f + jnp.einsum('rf,df->rd', grad_pre.astype(jnp.float32), weight_in.astype(jnp.float32))).astype(jnp.bfloat16)
    return (grad_in, grad_out, grad_x)

def reference(inputs, targets, w_in, w_out):
    loss_scale = 1.0 / math.sqrt(MICRO * BROWS)

    def one_micro(carry_in, pair_in):
        first_act, target_now = pair_in

        def forward_step(act_in, weights):
            hidden, act_out = cell_forward(act_in, weights[0], weights[1])
            return (act_out, (act_in, hidden))
        last_act, (stash_act, stash_hidden) = lax.scan(forward_step, first_act, (w_in, w_out))
        grad_top = ((last_act.astype(jnp.float32) - target_now.astype(jnp.float32)) * loss_scale).astype(jnp.bfloat16)

        def backward_step(grad_y, items):
            act_in, hidden, weight_in, weight_out = items
            grad_in, grad_out, grad_x = cell_backward(act_in, hidden, grad_y, weight_in, weight_out)
            return (grad_x, (grad_in, grad_out))
        unused_grad, (grads_in, grads_out) = lax.scan(backward_step, grad_top, (stash_act, stash_hidden, w_in, w_out), reverse=True)
        return ((carry_in[0] + grads_in, carry_in[1] + grads_out), None)
    zero_in = jnp.zeros(w_in.shape, jnp.float32)
    zero_out = jnp.zeros(w_out.shape, jnp.float32)
    (total_in, total_out), unused_out = lax.scan(one_micro, (zero_in, zero_out), (inputs, targets))
    return (total_in, total_out)
```

```python
import functools
import math

import jax
import jax.numpy as jnp
from jax import lax
from jax.experimental import pallas as pl
from jax.experimental.pallas import tpu as pltpu
from jax.sharding import PartitionSpec as P

WINDOW = 4
TILE = 512
VMEM_LIMIT = 12 * 1024 * 1024


def sigmoid(x):
    return 0.5 * jnp.tanh(0.5 * x) + 0.5


def forward_kernel(act_ref, win_ref, wout_ref, out_ref):
    act = act_ref[...]
    steps = win_ref.shape[1] // TILE

    def step(j, total):
        cols = pl.ds(pl.multiple_of(j * TILE, TILE), TILE)
        pre = jnp.dot(act, win_ref[:, cols], preferred_element_type=jnp.float32)
        hidden = (pre * sigmoid(pre)).astype(jnp.bfloat16)
        return total + jnp.dot(hidden, wout_ref[cols, :], preferred_element_type=jnp.float32)

    total = lax.fori_loop(0, steps, step, act.astype(jnp.float32), unroll=2)
    out_ref[...] = total.astype(jnp.bfloat16)


def backward_kernel(tick, sections, sec_ref, grad_ref, wout_t_ref, win_t_ref, slope_ref, out_ref):
    grad = grad_ref[...]
    steps = wout_t_ref.shape[1] // TILE
    slot = jnp.clip(tick - (sections - 1) + sec_ref[0], 0, slope_ref.shape[0] - 1)

    def step(j, total):
        cols = pl.ds(pl.multiple_of(j * TILE, TILE), TILE)
        through = jnp.dot(grad, wout_t_ref[:, cols], preferred_element_type=jnp.float32)
        grad_pre = (through * slope_ref[slot, :, cols]).astype(jnp.bfloat16)
        return total + jnp.dot(grad_pre, win_t_ref[cols, :], preferred_element_type=jnp.float32)

    total = lax.fori_loop(0, steps, step, grad.astype(jnp.float32), unroll=2)
    out_ref[...] = total.astype(jnp.bfloat16)


def slope_kernel(act_ref, win_ref, slope_ref):
    steps = win_ref.shape[1] // TILE

    def step(j, carry):
        cols = pl.ds(pl.multiple_of(j * TILE, TILE), TILE)
        for slot in range(act_ref.shape[0]):
            pre = jnp.dot(act_ref[slot], win_ref[:, cols], preferred_element_type=jnp.float32)
            sig = sigmoid(pre)
            slope_ref[slot, :, cols] = sig + pre * sig * (1.0 - sig)
        return carry

    lax.fori_loop(0, steps, step, 0)


def in_vmem():
    return pl.BlockSpec(memory_space=pltpu.VMEM)


def per_device(inputs, targets, w_in, w_out):
    sections = lax.axis_size("section")
    shares = lax.axis_size("dp")
    sec = lax.axis_index("section")
    share = lax.axis_index("dp")
    micro, rows, width = inputs.shape
    hidden_dim = w_in.shape[2]
    loss_scale = 1.0 / math.sqrt(micro * rows * shares)
    chunk = micro * rows // WINDOW
    inputs = inputs.reshape(WINDOW, chunk, width)
    targets = targets.reshape(WINDOW, chunk, width)
    weight_in, weight_out = w_in[0], w_out[0]
    is_first = sec == 0
    is_last = sec == sections - 1
    sec_arr = sec.astype(jnp.int32).reshape(1)
    params = pltpu.CompilerParams(vmem_limit_bytes=VMEM_LIMIT)
    rows_shape = jax.ShapeDtypeStruct((chunk, width), jnp.bfloat16)

    forward = pl.pallas_call(
        forward_kernel,
        out_shape=rows_shape,
        in_specs=[in_vmem()] * 3,
        out_specs=in_vmem(),
        compiler_params=params,
        name="fwd",
    )
    slope_of = pl.pallas_call(
        slope_kernel,
        out_shape=jax.ShapeDtypeStruct((WINDOW, chunk, hidden_dim), jnp.float32),
        in_specs=[in_vmem()] * 2,
        out_specs=in_vmem(),
        compiler_params=params,
        name="slope",
    )

    def backward(tick):
        return pl.pallas_call(
            functools.partial(backward_kernel, tick, sections),
            out_shape=rows_shape,
            in_specs=[pl.BlockSpec(memory_space=pltpu.SMEM)] + [in_vmem()] * 4,
            out_specs=in_vmem(),
            compiler_params=params,
            name="bwd",
        )

    ticks = sections + WINDOW - 1
    received = []
    tops = []
    act = jnp.where(is_first, inputs[0], jnp.zeros_like(inputs[0]))
    for tick in range(ticks):
        out = forward(act, weight_in, weight_out)
        if tick >= sections - 1:
            tops.append(out)
        if tick < ticks - 1:
            pairs = [(s, s + 1) for s in range(sections - 1) if 0 <= tick - s < WINDOW]
            act = lax.ppermute(out, "section", pairs)
            received.append(act)
            if tick + 1 < WINDOW:
                act = jnp.where(is_first, inputs[tick + 1], act)
    acts = jnp.where(
        is_first,
        inputs,
        lax.dynamic_slice_in_dim(jnp.stack(received), jnp.maximum(sec - 1, 0), WINDOW, 0),
    )
    slopes = slope_of(acts, weight_in)
    top_grad = (
        (jnp.stack(tops).astype(jnp.float32) - targets.astype(jnp.float32)) * loss_scale
    ).astype(jnp.bfloat16)

    weight_in_t, weight_out_t = weight_in.T, weight_out.T
    arrived = []
    grad = jnp.where(is_last, top_grad[0], jnp.zeros_like(top_grad[0]))
    for tick in range(ticks - 1):
        out = backward(tick)(sec_arr, grad, weight_out_t, weight_in_t, slopes)
        pairs = [(s, s - 1) for s in range(1, sections) if 0 <= tick - (sections - 1 - s) < WINDOW]
        grad = lax.ppermute(out, "section", pairs)
        arrived.append(grad)
        if tick + 1 < WINDOW:
            grad = jnp.where(is_last, top_grad[tick + 1], grad)
    start = jnp.maximum(sections - 2 - sec, 0)
    grads = jnp.where(
        is_last, top_grad, lax.dynamic_slice_in_dim(jnp.stack(arrived), start, WINDOW, 0)
    )

    all_acts = lax.all_gather(acts.reshape(micro * rows, width), "dp", tiled=True)
    all_grads = lax.all_gather(grads.reshape(micro * rows, width), "dp", tiled=True)
    part = hidden_dim // shares
    in_part = lax.dynamic_slice_in_dim(weight_in, share * part, part, 1)
    out_part = lax.dynamic_slice_in_dim(weight_out, share * part, part, 0)
    pre = jnp.dot(all_acts, in_part, preferred_element_type=jnp.float32)
    sig = sigmoid(pre)
    hidden = (pre * sig).astype(jnp.bfloat16)
    slope = sig + pre * sig * (1.0 - sig)
    through = jnp.einsum("rd,fd->rf", all_grads, out_part, preferred_element_type=jnp.float32)
    grad_pre = (through * slope).astype(jnp.bfloat16)
    share_in = jnp.einsum("rd,rf->df", all_acts, grad_pre, preferred_element_type=jnp.float32)
    share_out = jnp.einsum("rf,rd->fd", hidden, all_grads, preferred_element_type=jnp.float32)
    return (share_in[None], share_out[None])


def solution(mesh):
    in_specs = (
        P(None, "dp", None),
        P(None, "dp", None),
        P("section", None, None),
        P("section", None, None),
    )
    out_specs = (P("section", None, "dp"), P("section", "dp", None))
    return jax.shard_map(
        per_device, mesh=mesh, in_specs=in_specs, out_specs=out_specs, check_vma=False
    )
```

```python
import functools
import math

import jax
import jax.numpy as jnp
from jax import lax
from jax.experimental import pallas as pl
from jax.experimental.pallas import tpu as pltpu
from jax.sharding import PartitionSpec as P

WINDOW = 4
TILE = 1024
PARTS = 4
VMEM_LIMIT = 12 * 1024 * 1024


def sigmoid(x):
    return 0.5 * jnp.tanh(0.5 * x) + 0.5


def forward_kernel(act_ref, win_ref, wout_ref, out_ref):
    act = act_ref[...]
    total = act.astype(jnp.float32)
    for low in range(0, win_ref.shape[1], TILE):
        cols = slice(low, low + TILE)
        pre = jnp.dot(act, win_ref[:, cols], preferred_element_type=jnp.float32)
        hidden = (pre * sigmoid(pre)).astype(jnp.bfloat16)
        total = total + jnp.dot(hidden, wout_ref[cols, :], preferred_element_type=jnp.float32)
    out_ref[...] = total.astype(jnp.bfloat16)


def backward_kernel(tick, sections, sec_ref, grad_ref, slope_ref, *refs):
    weights, out_ref = refs[:-1], refs[-1]
    count = len(weights) // 2
    grad = grad_ref[...]
    total = grad.astype(jnp.float32)
    slot = jnp.clip(tick - (sections - 1) + sec_ref[0], 0, slope_ref.shape[0] - 1)
    part = weights[0].shape[1]
    for n in range(count):
        through = jnp.dot(grad, weights[n][...], preferred_element_type=jnp.float32)
        slope = slope_ref[slot, :, n * part : (n + 1) * part]
        grad_pre = (through * slope).astype(jnp.bfloat16)
        total = total + jnp.dot(
            grad_pre, weights[count + n][...], preferred_element_type=jnp.float32
        )
    out_ref[...] = total.astype(jnp.bfloat16)


def slope_kernel(act_ref, win_ref, slope_ref):
    slots, chunk, width = act_ref.shape
    act = act_ref[...].reshape(slots * chunk, width)
    steps = win_ref.shape[1] // 512

    def step(j, carry):
        cols = pl.ds(pl.multiple_of(j * 512, 512), 512)
        pre = jnp.dot(act, win_ref[:, cols], preferred_element_type=jnp.float32)
        sig = sigmoid(pre)
        slope = sig + pre * sig * (1.0 - sig)
        slope_ref[:, :, cols] = slope.reshape(slots, chunk, 512)
        return carry

    lax.fori_loop(0, steps, step, 0, unroll=2)


def turn_kernel(low, size, dim, after_ref, weight_ref, out_ref):
    if dim == 0:
        out_ref[...] = weight_ref[low : low + size, :].T
    else:
        out_ref[...] = weight_ref[:, low : low + size].T


def sending(tick):
    base = tick - tick % 2
    return range(base - WINDOW + 1, base + 2)


def in_vmem():
    return pl.BlockSpec(memory_space=pltpu.VMEM)


def per_device(inputs, targets, w_in, w_out):
    sections = lax.axis_size("section")
    shares = lax.axis_size("dp")
    sec = lax.axis_index("section")
    share = lax.axis_index("dp")
    micro, rows, width = inputs.shape
    hidden_dim = w_in.shape[2]
    loss_scale = 1.0 / math.sqrt(micro * rows * shares)
    chunk = micro * rows // WINDOW
    inputs = inputs.reshape(WINDOW, chunk, width)
    targets = targets.reshape(WINDOW, chunk, width)
    weight_in, weight_out = w_in[0], w_out[0]
    is_first = sec == 0
    is_last = sec == sections - 1
    sec_arr = sec.astype(jnp.int32).reshape(1)
    params = pltpu.CompilerParams(vmem_limit_bytes=VMEM_LIMIT)
    rows_shape = jax.ShapeDtypeStruct((chunk, width), jnp.bfloat16)

    forward = pl.pallas_call(
        forward_kernel,
        out_shape=rows_shape,
        in_specs=[in_vmem()] * 3,
        out_specs=in_vmem(),
        compiler_params=params,
        name="fwd",
    )
    slope_of = pl.pallas_call(
        slope_kernel,
        out_shape=jax.ShapeDtypeStruct((WINDOW, chunk, hidden_dim), jnp.float32),
        in_specs=[in_vmem()] * 2,
        out_specs=in_vmem(),
        compiler_params=params,
        name="slope",
    )

    def backward(tick):
        return pl.pallas_call(
            functools.partial(backward_kernel, tick, sections),
            out_shape=rows_shape,
            in_specs=[pl.BlockSpec(memory_space=pltpu.SMEM)] + [in_vmem()] * (2 + 2 * PARTS),
            out_specs=in_vmem(),
            compiler_params=params,
            name="bwd",
        )

    piece = hidden_dim // PARTS

    def turned_part(low, dim):
        shape = (width, piece) if dim == 0 else (piece, width)
        return pl.pallas_call(
            functools.partial(turn_kernel, low, piece, dim),
            out_shape=jax.ShapeDtypeStruct(shape, jnp.bfloat16),
            in_specs=[pl.BlockSpec(memory_space=pl.ANY), in_vmem()],
            out_specs=in_vmem(),
            compiler_params=params,
            name="turn",
        )

    ticks = sections + WINDOW - 1
    act_start = jnp.maximum(sec - 1, 0).astype(jnp.uint32)
    grad_start = jnp.maximum(sections - 2 - sec, 0).astype(jnp.uint32)
    part = hidden_dim // shares
    share_start = (share * part).astype(jnp.uint32)
    act = jnp.where(is_first, inputs[0], jnp.zeros_like(inputs[0]))
    act, sec_arr, act_start, grad_start, share_start, is_first, is_last = (
        lax.optimization_barrier(
            (act, sec_arr, act_start, grad_start, share_start, is_first, is_last)
        )
    )
    received = []
    tops = []
    turned = []
    for tick in range(ticks):
        out = forward(act, weight_in, weight_out)
        if tick >= sections - 1:
            tops.append(out)
        if tick < ticks - 1:
            pairs = [(s, s + 1) for s in sending(tick) if 0 <= s < sections - 1]
            act = lax.ppermute(out, "section", pairs)
            turn = tick - WINDOW
            if 0 <= turn < 2 * PARTS:
                low = turn % PARTS * piece
                if turn < PARTS:
                    block = turned_part(low, 0)(out, weight_out)
                else:
                    block = turned_part(low, 1)(out, weight_in)
                act, block = lax.optimization_barrier((act, block))
                turned.append(block)
            received.append(act)
            if tick + 1 < WINDOW:
                act = jnp.where(is_first, inputs[tick + 1], act)
    acts = jnp.where(
        is_first,
        inputs,
        lax.dynamic_slice_in_dim(jnp.stack(received), act_start, WINDOW, 0),
    )
    slopes = slope_of(acts, weight_in)
    top_grad = (
        (jnp.stack(tops).astype(jnp.float32) - targets.astype(jnp.float32)) * loss_scale
    ).astype(jnp.bfloat16)

    arrived = []
    grad = jnp.where(is_last, top_grad[0], jnp.zeros_like(top_grad[0]))
    for tick in range(ticks - 1):
        out = backward(tick)(sec_arr, grad, slopes, *turned)
        pairs = [(sections - 1 - k, sections - 2 - k) for k in sending(tick) if 0 <= k < sections - 1]
        grad = lax.ppermute(out, "section", pairs)
        arrived.append(grad)
        if tick + 1 < WINDOW:
            grad = jnp.where(is_last, top_grad[tick + 1], grad)

    in_part = lax.dynamic_slice_in_dim(weight_in, share_start, part, 1)
    out_part = lax.dynamic_slice_in_dim(weight_out, share_start, part, 0)
    grads = jnp.where(
        is_last,
        top_grad,
        lax.dynamic_slice_in_dim(jnp.stack(arrived), grad_start, WINDOW, 0),
    )
    all_acts = lax.all_gather(acts.reshape(micro * rows, width), "dp", tiled=True)
    all_grads = lax.all_gather(grads.reshape(micro * rows, width), "dp", tiled=True)
    pre = jnp.dot(all_acts, in_part, preferred_element_type=jnp.float32)
    sig = sigmoid(pre)
    hidden = (pre * sig).astype(jnp.bfloat16)
    slope = sig + pre * sig * (1.0 - sig)
    through = jnp.einsum("rd,fd->rf", all_grads, out_part, preferred_element_type=jnp.float32)
    grad_pre = (through * slope).astype(jnp.bfloat16)
    share_in = jnp.einsum("rd,rf->df", all_acts, grad_pre, preferred_element_type=jnp.float32)
    share_out = jnp.einsum("rf,rd->fd", hidden, all_grads, preferred_element_type=jnp.float32)
    return (share_in[None], share_out[None])


def solution(mesh):
    in_specs = (
        P(None, "dp", None),
        P(None, "dp", None),
        P("section", None, None),
        P("section", None, None),
    )
    out_specs = (P("section", None, "dp"), P("section", "dp", None))
    return jax.shard_map(
        per_device, mesh=mesh, in_specs=in_specs, out_specs=out_specs, check_vma=False
    )
```

```python
import functools
import math

import jax
import jax.numpy as jnp
from jax import lax
from jax.experimental import pallas as pl
from jax.experimental.pallas import tpu as pltpu
from jax.sharding import PartitionSpec as P

STREAMS = 2
ROUNDS = 2
SHARED = 4
WINDOW = STREAMS * ROUNDS
TILE = 1024
PARTS = 4
VMEM_LIMIT = 12 * 1024 * 1024


def sigmoid(x):
    return 0.5 * jnp.tanh(0.5 * x) + 0.5


def forward_kernel(act_ref, win_ref, wout_ref, out_ref):
    act = act_ref[...]
    total = act.astype(jnp.float32)
    for low in range(0, win_ref.shape[1], TILE):
        cols = slice(low, low + TILE)
        pre = jnp.dot(act, win_ref[:, cols], preferred_element_type=jnp.float32)
        hidden = (pre * sigmoid(pre)).astype(jnp.bfloat16)
        total = total + jnp.dot(hidden, wout_ref[cols, :], preferred_element_type=jnp.float32)
    out_ref[...] = total.astype(jnp.bfloat16)


def backward_kernel(tick, stream, sections, sec_ref, grad_ref, slope_ref, *refs):
    weights, out_ref = refs[:-1], refs[-1]
    count = len(weights) // 2
    grad = grad_ref[...]
    total = grad.astype(jnp.float32)
    turn = jnp.clip(tick - (sections - 1) + sec_ref[0], 0, ROUNDS - 1)
    slot = turn * STREAMS + stream
    part = weights[0].shape[1]
    for n in range(count):
        through = jnp.dot(grad, weights[n][...], preferred_element_type=jnp.float32)
        slope = slope_ref[slot, :, n * part : (n + 1) * part]
        grad_pre = (through * slope).astype(jnp.bfloat16)
        total = total + jnp.dot(
            grad_pre, weights[count + n][...], preferred_element_type=jnp.float32
        )
    out_ref[...] = total.astype(jnp.bfloat16)


def slope_kernel(act_ref, win_ref, slope_ref):
    slots, chunk, width = act_ref.shape
    act = act_ref[...].reshape(slots * chunk, width)
    steps = win_ref.shape[1] // 512

    def step(j, carry):
        cols = pl.ds(pl.multiple_of(j * 512, 512), 512)
        pre = jnp.dot(act, win_ref[:, cols], preferred_element_type=jnp.float32)
        sig = sigmoid(pre)
        slope = sig + pre * sig * (1.0 - sig)
        slope_ref[:, :, cols] = slope.reshape(slots, chunk, 512)
        return carry

    lax.fori_loop(0, steps, step, 0, unroll=2)


def turn_kernel(low, size, dim, after_ref, weight_ref, out_ref):
    if dim == 0:
        out_ref[...] = weight_ref[low : low + size, :].T
    else:
        out_ref[...] = weight_ref[:, low : low + size].T


def sending(tick):
    base = tick - tick % SHARED
    return range(base - ROUNDS + 1, base + SHARED)


def in_vmem():
    return pl.BlockSpec(memory_space=pltpu.VMEM)


def per_device(inputs, targets, w_in, w_out):
    sections = lax.axis_size("section")
    shares = lax.axis_size("dp")
    sec = lax.axis_index("section")
    share = lax.axis_index("dp")
    micro, rows, width = inputs.shape
    hidden_dim = w_in.shape[2]
    loss_scale = 1.0 / math.sqrt(micro * rows * shares)
    chunk = micro * rows // WINDOW
    inputs = inputs.reshape(WINDOW, chunk, width)
    targets = targets.reshape(WINDOW, chunk, width)
    weight_in, weight_out = w_in[0], w_out[0]
    is_first = sec == 0
    is_last = sec == sections - 1
    sec_arr = sec.astype(jnp.int32).reshape(1)
    params = pltpu.CompilerParams(vmem_limit_bytes=VMEM_LIMIT)
    rows_shape = jax.ShapeDtypeStruct((chunk, width), jnp.bfloat16)

    forward = pl.pallas_call(
        forward_kernel,
        out_shape=rows_shape,
        in_specs=[in_vmem()] * 3,
        out_specs=in_vmem(),
        compiler_params=params,
        name="fwd",
    )
    slope_of = pl.pallas_call(
        slope_kernel,
        out_shape=jax.ShapeDtypeStruct((WINDOW, chunk, hidden_dim), jnp.float32),
        in_specs=[in_vmem()] * 2,
        out_specs=in_vmem(),
        compiler_params=params,
        name="slope",
    )

    def backward(tick, stream):
        return pl.pallas_call(
            functools.partial(backward_kernel, tick, stream, sections),
            out_shape=rows_shape,
            in_specs=[pl.BlockSpec(memory_space=pltpu.SMEM)] + [in_vmem()] * (2 + 2 * PARTS),
            out_specs=in_vmem(),
            compiler_params=params,
            name="bwd",
        )

    piece = hidden_dim // PARTS

    def turned_part(low, dim):
        shape = (width, piece) if dim == 0 else (piece, width)
        return pl.pallas_call(
            functools.partial(turn_kernel, low, piece, dim),
            out_shape=jax.ShapeDtypeStruct(shape, jnp.bfloat16),
            in_specs=[pl.BlockSpec(memory_space=pl.ANY), in_vmem()],
            out_specs=in_vmem(),
            compiler_params=params,
            name="turn",
        )

    ticks = sections + ROUNDS - 1
    streams = range(STREAMS)
    act_start = jnp.maximum(sec - 1, 0).astype(jnp.uint32)
    grad_start = jnp.maximum(sections - 2 - sec, 0).astype(jnp.uint32)
    part = hidden_dim // shares
    share_start = (share * part).astype(jnp.uint32)
    act = [jnp.where(is_first, inputs[n], jnp.zeros_like(inputs[n])) for n in streams]
    act, sec_arr, act_start, grad_start, share_start, is_first, is_last = (
        lax.optimization_barrier(
            (act, sec_arr, act_start, grad_start, share_start, is_first, is_last)
        )
    )
    received = [[] for _ in streams]
    tops = []
    turned = []
    for tick in range(ticks):
        for n in streams:
            out = forward(act[n], weight_in, weight_out)
            if tick >= sections - 1:
                tops.append(out)
            if tick < ticks - 1:
                pairs = [(s, s + 1) for s in sending(tick) if 0 <= s < sections - 1]
                act[n] = lax.ppermute(out, "section", pairs)
                turn = tick - ROUNDS
                if n == 0 and 0 <= turn < 2 * PARTS:
                    low = turn % PARTS * piece
                    if turn < PARTS:
                        block = turned_part(low, 0)(out, weight_out)
                    else:
                        block = turned_part(low, 1)(out, weight_in)
                    act[n], block = lax.optimization_barrier((act[n], block))
                    turned.append(block)
                received[n].append(act[n])
                if tick + 1 < ROUNDS:
                    act[n] = jnp.where(is_first, inputs[(tick + 1) * STREAMS + n], act[n])

    def picked(buffers, start, low, count):
        slices = [
            lax.dynamic_slice_in_dim(jnp.stack(buffers[n]), start + low, count, 0)
            for n in streams
        ]
        return jnp.stack(slices, 1).reshape(count * STREAMS, chunk, width)

    acts = jnp.where(is_first, inputs, picked(received, act_start, jnp.uint32(0), ROUNDS))
    slopes = slope_of(acts, weight_in)
    top_grad = (
        (jnp.stack(tops).astype(jnp.float32) - targets.astype(jnp.float32)) * loss_scale
    ).astype(jnp.bfloat16)

    arrived = [[] for _ in streams]
    grad = [jnp.where(is_last, top_grad[n], jnp.zeros_like(top_grad[n])) for n in streams]
    for tick in range(ticks - 1):
        pairs = [
            (sections - 1 - k, sections - 2 - k) for k in sending(tick) if 0 <= k < sections - 1
        ]
        for n in streams:
            out = backward(tick, n)(sec_arr, grad[n], slopes, *turned)
            grad[n] = lax.ppermute(out, "section", pairs)
            arrived[n].append(grad[n])
            if tick + 1 < ROUNDS:
                grad[n] = jnp.where(is_last, top_grad[(tick + 1) * STREAMS + n], grad[n])

    in_part = lax.dynamic_slice_in_dim(weight_in, share_start, part, 1)
    out_part = lax.dynamic_slice_in_dim(weight_out, share_start, part, 0)
    grads = jnp.where(is_last, top_grad, picked(arrived, grad_start, jnp.uint32(0), ROUNDS))
    all_acts = lax.all_gather(acts.reshape(-1, width), "dp", tiled=True)
    all_grads = lax.all_gather(grads.reshape(-1, width), "dp", tiled=True)
    pre = jnp.dot(all_acts, in_part, preferred_element_type=jnp.float32)
    sig = sigmoid(pre)
    hidden = (pre * sig).astype(jnp.bfloat16)
    slope = sig + pre * sig * (1.0 - sig)
    through = jnp.einsum("rd,fd->rf", all_grads, out_part, preferred_element_type=jnp.float32)
    grad_pre = (through * slope).astype(jnp.bfloat16)
    share_in = jnp.einsum("rd,rf->df", all_acts, grad_pre, preferred_element_type=jnp.float32)
    share_out = jnp.einsum("rf,rd->fd", hidden, all_grads, preferred_element_type=jnp.float32)
    return (share_in[None], share_out[None])


def solution(mesh):
    in_specs = (
        P(None, "dp", None),
        P(None, "dp", None),
        P("section", None, None),
        P("section", None, None),
    )
    out_specs = (P("section", None, "dp"), P("section", "dp", None))
    return jax.shard_map(
        per_device, mesh=mesh, in_specs=in_specs, out_specs=out_specs, check_vma=False
    )
```

```python
import functools
import math

import jax
import jax.numpy as jnp
from jax import lax
from jax.experimental import pallas as pl
from jax.experimental.pallas import tpu as pltpu
from jax.sharding import PartitionSpec as P

WINDOW = 4
TILE = 1024
PARTS = 4
VMEM_LIMIT = 12 * 1024 * 1024


def sigmoid(x):
    return 0.5 * jnp.tanh(0.5 * x) + 0.5


def forward_kernel(act_ref, win_ref, wout_ref, out_ref):
    act = act_ref[...]
    total = act.astype(jnp.float32)
    for low in range(0, win_ref.shape[1], TILE):
        cols = slice(low, low + TILE)
        pre = jnp.dot(act, win_ref[:, cols], preferred_element_type=jnp.float32)
        hidden = (pre * sigmoid(pre)).astype(jnp.bfloat16)
        total = total + jnp.dot(hidden, wout_ref[cols, :], preferred_element_type=jnp.float32)
    out_ref[...] = total.astype(jnp.bfloat16)


def backward_kernel(tick, sections, sec_ref, grad_ref, slope_ref, *refs):
    weights, out_ref = refs[:-1], refs[-1]
    count = len(weights) // 2
    grad = grad_ref[...]
    total = grad.astype(jnp.float32)
    slot = jnp.clip(tick - (sections - 1) + sec_ref[0], 0, slope_ref.shape[0] - 1)
    part = weights[0].shape[1]
    for n in range(count):
        through = jnp.dot(grad, weights[n][...], preferred_element_type=jnp.float32)
        slope = slope_ref[slot, :, n * part : (n + 1) * part]
        grad_pre = (through * slope).astype(jnp.bfloat16)
        total = total + jnp.dot(
            grad_pre, weights[count + n][...], preferred_element_type=jnp.float32
        )
    out_ref[...] = total.astype(jnp.bfloat16)


def slope_kernel(act_ref, win_ref, slope_ref):
    slots, chunk, width = act_ref.shape
    act = act_ref[...].reshape(slots * chunk, width)
    steps = win_ref.shape[1] // 512

    def step(j, carry):
        cols = pl.ds(pl.multiple_of(j * 512, 512), 512)
        pre = jnp.dot(act, win_ref[:, cols], preferred_element_type=jnp.float32)
        sig = sigmoid(pre)
        slope = sig + pre * sig * (1.0 - sig)
        slope_ref[:, :, cols] = slope.reshape(slots, chunk, 512)
        return carry

    lax.fori_loop(0, steps, step, 0, unroll=2)


def turn_kernel(low, size, dim, after_ref, weight_ref, out_ref):
    if dim == 0:
        out_ref[...] = weight_ref[low : low + size, :].T
    else:
        out_ref[...] = weight_ref[:, low : low + size].T


def sending(tick):
    base = tick - tick % 2
    return range(base - WINDOW + 1, base + 2)


def in_vmem():
    return pl.BlockSpec(memory_space=pltpu.VMEM)


def per_device(inputs, targets, w_in, w_out):
    sections = lax.axis_size("section")
    shares = lax.axis_size("dp")
    sec = lax.axis_index("section")
    share = lax.axis_index("dp")
    micro, rows, width = inputs.shape
    hidden_dim = w_in.shape[2]
    loss_scale = 1.0 / math.sqrt(micro * rows * shares)
    chunk = micro * rows // WINDOW
    inputs = inputs.reshape(WINDOW, chunk, width)
    targets = targets.reshape(WINDOW, chunk, width)
    weight_in, weight_out = w_in[0], w_out[0]
    is_first = sec == 0
    is_last = sec == sections - 1
    sec_arr = sec.astype(jnp.int32).reshape(1)
    params = pltpu.CompilerParams(vmem_limit_bytes=VMEM_LIMIT)
    rows_shape = jax.ShapeDtypeStruct((chunk, width), jnp.bfloat16)

    forward = pl.pallas_call(
        forward_kernel,
        out_shape=rows_shape,
        in_specs=[in_vmem()] * 3,
        out_specs=in_vmem(),
        compiler_params=params,
        name="fwd",
    )
    slope_of = pl.pallas_call(
        slope_kernel,
        out_shape=jax.ShapeDtypeStruct((WINDOW, chunk, hidden_dim), jnp.float32),
        in_specs=[in_vmem()] * 2,
        out_specs=in_vmem(),
        compiler_params=params,
        name="slope",
    )

    def backward(tick):
        return pl.pallas_call(
            functools.partial(backward_kernel, tick, sections),
            out_shape=rows_shape,
            in_specs=[pl.BlockSpec(memory_space=pltpu.SMEM)] + [in_vmem()] * (2 + 2 * PARTS),
            out_specs=in_vmem(),
            compiler_params=params,
            name="bwd",
        )

    piece = hidden_dim // PARTS

    def turned_part(low, dim):
        shape = (width, piece) if dim == 0 else (piece, width)
        return pl.pallas_call(
            functools.partial(turn_kernel, low, piece, dim),
            out_shape=jax.ShapeDtypeStruct(shape, jnp.bfloat16),
            in_specs=[pl.BlockSpec(memory_space=pl.ANY), in_vmem()],
            out_specs=in_vmem(),
            compiler_params=params,
            name="turn",
        )

    ticks = sections + WINDOW - 1
    act_start = jnp.maximum(sec - 1, 0).astype(jnp.uint32)
    grad_start = jnp.maximum(sections - 2 - sec, 0).astype(jnp.uint32)
    part = hidden_dim // shares
    share_start = (share * part).astype(jnp.uint32)
    act = jnp.where(is_first, inputs[0], jnp.zeros_like(inputs[0]))
    act, sec_arr, act_start, grad_start, share_start, is_first, is_last = (
        lax.optimization_barrier(
            (act, sec_arr, act_start, grad_start, share_start, is_first, is_last)
        )
    )
    received = []
    tops = []
    turned = []
    for tick in range(ticks):
        out = forward(act, weight_in, weight_out)
        if tick >= sections - 1:
            tops.append(out)
        if tick < ticks - 1:
            pairs = [(s, s + 1) for s in sending(tick) if 0 <= s < sections - 1]
            act = lax.ppermute(out, "section", pairs)
            turn = tick - WINDOW
            if 0 <= turn < 2 * PARTS:
                low = turn % PARTS * piece
                if turn < PARTS:
                    block = turned_part(low, 0)(out, weight_out)
                else:
                    block = turned_part(low, 1)(out, weight_in)
                act, block = lax.optimization_barrier((act, block))
                turned.append(block)
            received.append(act)
            if tick + 1 < WINDOW:
                act = jnp.where(is_first, inputs[tick + 1], act)
    acts = jnp.where(
        is_first,
        inputs,
        lax.dynamic_slice_in_dim(jnp.stack(received), act_start, WINDOW, 0),
    )
    slopes = slope_of(acts, weight_in)
    top_grad = (
        (jnp.stack(tops).astype(jnp.float32) - targets.astype(jnp.float32)) * loss_scale
    ).astype(jnp.bfloat16)

    arrived = []
    grad = jnp.where(is_last, top_grad[0], jnp.zeros_like(top_grad[0]))
    for tick in range(ticks - 1):
        out = backward(tick)(sec_arr, grad, slopes, *turned)
        pairs = [(sections - 1 - k, sections - 2 - k) for k in sending(tick) if 0 <= k < sections - 1]
        grad = lax.ppermute(out, "section", pairs)
        arrived.append(grad)
        if tick + 1 < WINDOW:
            grad = jnp.where(is_last, top_grad[tick + 1], grad)

    in_part = lax.dynamic_slice_in_dim(weight_in, share_start, part, 1)
    out_part = lax.dynamic_slice_in_dim(weight_out, share_start, part, 0)
    grads = jnp.where(
        is_last,
        top_grad,
        lax.dynamic_slice_in_dim(jnp.stack(arrived), grad_start, WINDOW, 0),
    )
    all_acts = lax.all_gather(acts.reshape(micro * rows, width), "dp", tiled=True)
    all_grads = lax.all_gather(grads.reshape(micro * rows, width), "dp", tiled=True)
    pre = jnp.dot(all_acts, in_part, preferred_element_type=jnp.float32)
    sig = sigmoid(pre)
    hidden = (pre * sig).astype(jnp.bfloat16)
    slope = sig + pre * sig * (1.0 - sig)
    hidden, slope = lax.optimization_barrier((hidden, slope))
    through = jnp.einsum("rd,fd->rf", all_grads, out_part, preferred_element_type=jnp.float32)
    grad_pre = (through * slope).astype(jnp.bfloat16)
    share_in = jnp.einsum("rd,rf->df", all_acts, grad_pre, preferred_element_type=jnp.float32)
    share_out = jnp.einsum("rf,rd->fd", hidden, all_grads, preferred_element_type=jnp.float32)
    return (share_in[None], share_out[None])


def solution(mesh):
    in_specs = (
        P(None, "dp", None),
        P(None, "dp", None),
        P("section", None, None),
        P("section", None, None),
    )
    out_specs = (P("section", None, "dp"), P("section", "dp", None))
    return jax.shard_map(
        per_device, mesh=mesh, in_specs=in_specs, out_specs=out_specs, check_vma=False
    )
```
